512 devices in a mesh: dp: 32 (over z_lo, y), mp: 16 (over x, z_hi, core).
Axes of the slice: x: 4, y: 4, z: 16 (z_hi: 2, z_lo: 8; z = z_hi * 8 + z_lo), core: 2. Of those that a mesh axis runs over, the one named last changes fastest.
Arguments:
- tokens: bfloat16 [32768, 8192], P('dp', 'mp'), may hold values from -6 to 6
- cotangent: bfloat16 [32768, 8192], P('dp', 'mp'), may hold values from -6 to 6
- first_factor: bfloat16 [64, 128, 128], P('mp'), may hold values from -0.5 to 0.5
- second_factor: bfloat16 [64, 128, 128], P('mp'), may hold values from -0.5 to 0.5
Outputs:
- output: bfloat16 [32768, 8192], P('dp', 'mp')
- input_grad: bfloat16 [32768, 8192], P('dp', 'mp')
- first_grad: float32 [64, 128, 128], P('mp')
- second_grad: float32 [64, 128, 128], P('mp')
The draws below stay inside these ranges and needn't reach their ends.
All inputs are finite; a program needn't handle non-finite values.
Results may differ from the reference program's by a relative error of at most 0.007.
Values may be sent and summed in bfloat16 or wider, within the bound.
A program may use at most 64 MiB of HBM per device.

```python
import jax
import jax.numpy as jnp
from jax import lax

NBLK = 64
BLK = 128
TOK_DEV = 1024
D = 8192
TOKENS = 32768
N_DP = 32


def block_levels(own_key, shape, shards, smallest, largest):
    loudness, own = 1.0, jax.random.fold_in(own_key, 6)
    for position, shards_of in shards:
        draws = jnp.exp(jax.random.uniform(jax.random.fold_in(own, position), (shards_of,), jnp.float32, smallest / len(shards), largest / len(shards)))
        loudness = loudness * jnp.repeat(draws, shape[position] // shards_of).reshape([-1 if axis == position else 1 for axis in range(len(shape))])
    return loudness


def scatter_about(rng, extent, deviation, limit, split=(), held_as=jnp.bfloat16):
    gain = block_levels(rng, extent, split, -0.22, 0.18) if split else 1.0
    values = jax.random.normal(rng, extent, jnp.float32) * deviation * gain
    return jnp.minimum(jnp.maximum(values, -limit), limit).astype(held_as)


def setup_inputs(seed: int = 0) -> dict:
    splits = jax.random.split(jax.random.key(seed), 5)
    tokens = scatter_about(splits[0], (TOKENS, D), 1.0, 6.0, ((0, 32), (1, 16)))
    cotangent = scatter_about(splits[1], (TOKENS, D), 1.0, 6.0, ((0, 32), (1, 16)))
    first_factor = scatter_about(splits[2], (NBLK, BLK, BLK), BLK ** -0.5, 0.5, ((0, 16),))
    second_factor = scatter_about(splits[3], (NBLK, BLK, BLK), BLK ** -0.5, 0.5, ((0, 16),))
    return dict(tokens=tokens, cotangent=cotangent, first_factor=first_factor, second_factor=second_factor)


def mult(form, left, right):
    return jnp.einsum(form, left.astype(jnp.float32), right.astype(jnp.float32), precision=lax.Precision.HIGHEST)

def reference(tokens, cotangent, first_factor, second_factor):
    ratio = BLK // NBLK
    w_first = first_factor.reshape(NBLK, BLK, NBLK, ratio)
    w_second = second_factor.reshape(NBLK, ratio, NBLK, NBLK, ratio)
    xs = tokens.reshape(N_DP, TOK_DEV, NBLK, BLK)
    gs = cotangent.reshape(N_DP, TOK_DEV, NBLK, BLK)

    def block(carry, pair):
        acc_first, acc_second = carry
        xb, gb = pair
        rows = xb.shape[0]
        hidden = mult('nix,ixjc->nijc', xb, w_first).astype(jnp.bfloat16)
        mixed = mult('nijc,jciab->najb', hidden, w_second).astype(jnp.bfloat16)
        zed = mixed.reshape(rows, NBLK, BLK).astype(jnp.float32)
        xf = xb.astype(jnp.float32)
        gf = gb.astype(jnp.float32)
        sig = jax.nn.sigmoid(xf)
        silu = xf * sig
        output = (zed * silu).astype(jnp.bfloat16)
        grad_z = (gf * silu).astype(jnp.bfloat16)
        gate_grad = (gf * zed * sig * (1.0 + xf * (1.0 - sig))).astype(jnp.bfloat16)
        grad_mixed = grad_z.reshape(rows, NBLK, NBLK, ratio)
        acc_second = acc_second + mult('nijc,najb->jciab', hidden, grad_mixed)
        grad_u = mult('najb,jciab->nijc', grad_mixed, w_second).astype(jnp.bfloat16)
        acc_first = acc_first + mult('nix,nijc->ixjc', xb, grad_u)
        input_grad = (mult('nijc,ixjc->nix', grad_u, w_first) + gate_grad.astype(jnp.float32)).astype(jnp.bfloat16)
        return ((acc_first, acc_second), (output, input_grad))
    start = (jnp.zeros((NBLK, BLK, NBLK, ratio), jnp.float32), jnp.zeros((NBLK, ratio, NBLK, NBLK, ratio), jnp.float32))
    (acc_first, acc_second), (outs, grads) = lax.scan(block, start, (xs, gs))
    scale = 1.0 / jnp.sqrt(jnp.float32(TOKENS))
    first_grad = acc_first.reshape(NBLK, BLK, BLK) * scale
    second_grad = acc_second.reshape(NBLK, BLK, BLK) * scale
    return (outs.reshape(TOKENS, D), grads.reshape(TOKENS, D), first_grad, second_grad)
```

```python
import jax
import jax.numpy as jnp
from jax import lax
from jax.experimental import pallas as pl
from jax.experimental.pallas import tpu as pltpu
from jax.sharding import PartitionSpec as P

MESH = pl.DeviceIdType.MESH
BF = jnp.bfloat16
F32 = jnp.float32
NT = (((1,), (1,)), ((), ()))
NN = (((1,), (0,)), ((), ()))


def dot(left, right, form=NN):
    return lax.dot_general(left, right, form, preferred_element_type=F32)


def iota(shape, axis):
    return lax.broadcasted_iota(jnp.int32, shape, axis)


def swap_matrix():
    row, col = iota((128, 128), 0), iota((128, 128), 1)
    source = (row & 0b1100111) + ((row & 8) << 1) + ((row & 16) >> 1)
    return (col == source).astype(BF)


def block_of(position, plane):
    above = position >> 5
    absolute = (above + plane) & 1
    return ((position >> 3) & 3) * 16 + absolute * 8 + (position & 7)


def column_ab(code, plane):
    return block_of(code >> 4, plane) * 2 + (code & 1)


def column_ci(code, plane):
    return (code & 1) * 64 + block_of(code >> 4, plane)


def kernel(
    chunks,
    tok, cot, w1, w2,
    out, grad_in, first_out, second_out,
    stage, held, back, landed, xt, gt, w1t, w1p, wpair, wf, wb, sel_ab, sel_ci, acc_first, acc_second, mid,
    send_a, recv_a, send_z, recv_z, send_b, recv_b, own_sem, w_sem,
):
    n = tok.shape[0] // chunks
    d, m = lax.axis_index("dp"), lax.axis_index("mp")
    x, plane, core = m // 4, (m // 2) % 2, m % 2
    me = x * 2 + core
    mate = (d, m + 2 - 4 * plane)

    def peer(k):
        q = (me + k) % 8
        return q, (d, (q // 2) * 4 + plane * 2 + q % 2)

    barrier = pltpu.get_barrier_semaphore()
    for k in range(1, 8):
        pl.semaphore_signal(barrier, inc=1, device_id=peer(k)[1], device_id_type=MESH)
    pl.semaphore_signal(barrier, inc=1, device_id=mate, device_id_type=MESH)

    def give_weights():
        return pltpu.make_async_remote_copy(
            w2, wpair.at[plane], w_sem.at[0], w_sem.at[1], device_id=mate, device_id_type=MESH
        )

    def keep_weights():
        return pltpu.make_async_copy(w2, wpair.at[plane], w_sem.at[2])

    def out_copy(c, k):
        q, device = peer(k)
        return pltpu.make_async_remote_copy(
            stage.at[c, q], held.at[c, 0, :, pl.ds(4 * me, 4)],
            send_a.at[c, k], recv_a.at[c, k], device_id=device, device_id_type=MESH,
        )

    def out_own(c):
        return pltpu.make_async_copy(stage.at[c, me], held.at[c, 0, :, pl.ds(4 * me, 4)], own_sem.at[c, 0])

    def plane_copy(c, kind):
        return pltpu.make_async_remote_copy(
            held.at[c, 0, kind], held.at[c, 1, kind],
            send_z.at[c, kind], recv_z.at[c, kind], device_id=mate, device_id_type=MESH,
        )

    def back_copy(c, k):
        q, device = peer(k)
        return pltpu.make_async_remote_copy(
            back.at[c, q], landed.at[c, :, :, me],
            send_b.at[c, k], recv_b.at[c, k], device_id=device, device_id_type=MESH,
        )

    def back_own(c):
        return pltpu.make_async_copy(back.at[c, me], landed.at[c, :, :, me], own_sem.at[c, 1])

    swap = swap_matrix()
    for i in range(4):
        half = dot(swap, w1[i], NT).astype(BF)
        w1t[i] = dot(half, swap).astype(BF)
        half = dot(swap, w1[i]).astype(BF)
        w1p[i] = dot(half, swap).astype(BF)
    acc_first[...] = jnp.zeros_like(acc_first)
    pl.semaphore_wait(barrier, 8)
    give_weights().start()
    keep_weights().start()

    def to_mate(c):
        for k in range(1, 8):
            out_copy(c, k).wait_recv()
        out_own(c).wait()
        for kind in range(2):
            plane_copy(c, kind).start()

    def begin(c, _):
        rows = pl.ds(pl.multiple_of(c * n, n), n)
        for i in range(4):
            cols = pl.ds(128 * i, 128)
            xf = dot(swap, tok[rows, cols], NT)
            gf = dot(swap, cot[rows, cols], NT)
            xb = xf.astype(BF)
            xt[c, i] = xb
            gt[c, i] = gf.astype(BF)
            hidden = dot(w1t[i], xb).astype(BF)
            grad_z = (gf * (xf * jax.nn.sigmoid(xf))).astype(BF)
            stage[c, :, 0, i] = hidden.reshape(8, 16, n)
            stage[c, :, 1, i] = grad_z.reshape(8, 16, n)
        out_own(c).start()
        for k in range(1, 8):
            out_copy(c, k).start()

        @pl.when(c >= 1)
        def _():
            to_mate(c - 1)

        return 0

    lax.fori_loop(0, chunks, begin, 0)
    to_mate(chunks - 1)

    rows_q, cols_q = iota((128, 1024), 0), iota((128, 1024), 1)
    sel_ab[...] = (rows_q == column_ab(cols_q, plane)).astype(BF)
    sel_ci[...] = (rows_q == column_ci(cols_q, plane)).astype(BF)
    give_weights().wait_recv()
    keep_weights().wait()

    def spread(b, _):
        start = pl.multiple_of(b * 128, 128)
        code = iota((128, 128), 0) + b * 128
        lane = iota((128, 128), 1)
        pick_ab = (lane == column_ab(code, plane)).astype(BF)
        pick_ci = (lane == column_ci(code, plane)).astype(BF)
        group = (code >> 1) & 7
        forward = jnp.zeros((128, 128), F32)
        backward = jnp.zeros((128, 128), F32)
        for j in range(8):
            block = wpair[j // 4, j % 4]
            forward = jnp.where(group == j, dot(pick_ab, block, NT), forward)
            backward = jnp.where(group == j, dot(pick_ci, block), backward)
        same = ((iota((128, 1024), 0) >> 1) & 7) == ((cols_q >> 1) & 7)
        wf[pl.ds(start, 128)] = jnp.where(same, dot(forward.astype(BF), sel_ci[...]), 0.0).astype(BF)
        wb[pl.ds(start, 128)] = jnp.where(same, dot(backward.astype(BF), sel_ab[...]), 0.0).astype(BF)
        return 0

    lax.fori_loop(0, 4, spread, 0)
    acc_second[...] = jnp.zeros_like(acc_second)
    eye = (iota((n, n), 0) == iota((n, n), 1)).astype(BF)

    def finish(c):
        for k in range(1, 8):
            back_copy(c, k).wait_recv()
        back_own(c).wait()
        rows = pl.ds(pl.multiple_of(c * n, n), n)
        for i in range(4):
            cols = pl.ds(128 * i, 128)
            xb = xt[c, i]
            xf = xb.astype(F32)
            gf = gt[c, i].astype(F32)
            zf = landed[c, 0, i].reshape(128, n).astype(F32)
            gu = landed[c, 1, i].reshape(128, n)
            sig = jax.nn.sigmoid(xf)
            y = (zf * (xf * sig)).astype(BF)
            gate = (gf * zf * sig * (1.0 + xf * (1.0 - sig))).astype(BF)
            gx = (dot(w1p[i], gu) + gate.astype(F32)).astype(BF)
            acc_first[i] += dot(xb, gu, NT)
            out[rows, cols] = dot(dot(eye, y, NT).astype(BF), swap).astype(BF)
            grad_in[rows, cols] = dot(dot(eye, gx, NT).astype(BF), swap).astype(BF)

    def middle(c, _):
        for kind in range(2):
            plane_copy(c, kind).wait_recv()
        hidden = held[c, :, 0].reshape(1024, n)
        grad_mixed = held[c, :, 1].reshape(1024, n)
        back[c, :, 0] = dot(wf[...], hidden).astype(BF).reshape(8, 4, 16, n)
        back[c, :, 1] = dot(wb[...], grad_mixed).astype(BF).reshape(8, 4, 16, n)
        back_own(c).start()
        for k in range(1, 8):
            back_copy(c, k).start()
        acc_second[...] += dot(hidden, grad_mixed, NT)

        @pl.when(c >= 1)
        def _():
            finish(c - 1)

        return 0

    lax.fori_loop(0, chunks, middle, 0)

    def gather(b, _):
        start = pl.multiple_of(b * 128, 128)
        code = iota((128, 1024), 0)
        same = ((code >> 1) & 7) == ((cols_q >> 1) & 7)
        part = jnp.where(same, acc_second[pl.ds(start, 128)], 0.0).astype(BF)
        mid[pl.ds(start, 128)] = dot(part, sel_ab[...], NT).astype(BF)
        return 0

    lax.fori_loop(0, 8, gather, 0)
    for j in range(4):
        chosen = ((cols_q >> 1) & 7) == plane * 4 + j
        pick = jnp.where(chosen, sel_ci[...].astype(F32), 0.0).astype(BF)
        second_out[j] = dot(pick, mid[...]).astype(BF)
    finish(chunks - 1)
    for i in range(4):
        half = dot(swap, acc_first[i].astype(BF)).astype(BF)
        first_out[i] = dot(half, swap).astype(BF)

    def drain(c, _):
        for k in range(1, 8):
            out_copy(c, k).wait_send()
            back_copy(c, k).wait_send()
        for kind in range(2):
            plane_copy(c, kind).wait_send()
        return 0

    lax.fori_loop(0, chunks, drain, 0)
    give_weights().wait_send()


def shards(tokens, cotangent, first_factor, second_factor):
    rows, width = tokens.shape
    chunks = 8
    n = rows // chunks
    V = pl.BlockSpec(memory_space=pltpu.VMEM)
    dma = pltpu.SemaphoreType.DMA
    small = jax.ShapeDtypeStruct(first_factor.shape, BF)
    wide = jax.ShapeDtypeStruct((rows, width), BF)
    output, input_grad, first, second = pl.pallas_call(
        lambda *refs: kernel(chunks, *refs),
        out_shape=(wide, wide, small, small),
        in_specs=[V] * 4,
        out_specs=(V,) * 4,
        scratch_shapes=[
            pltpu.VMEM((chunks, 8, 2, 4, 16, n), BF),
            pltpu.VMEM((chunks, 2, 2, 32, 16, n), BF),
            pltpu.VMEM((chunks, 8, 2, 4, 16, n), BF),
            pltpu.VMEM((chunks, 2, 4, 8, 16, n), BF),
            pltpu.VMEM((chunks, 4, 128, n), BF),
            pltpu.VMEM((chunks, 4, 128, n), BF),
            pltpu.VMEM((4, 128, 128), BF),
            pltpu.VMEM((4, 128, 128), BF),
            pltpu.VMEM((2, 4, 128, 128), BF),
            pltpu.VMEM((512, 1024), BF),
            pltpu.VMEM((512, 1024), BF),
            pltpu.VMEM((128, 1024), BF),
            pltpu.VMEM((128, 1024), BF),
            pltpu.VMEM((4, 128, 128), F32),
            pltpu.VMEM((1024, 1024), F32),
            pltpu.VMEM((1024, 128), BF),
            dma((chunks, 8)),
            dma((chunks, 8)),
            dma((chunks, 2)),
            dma((chunks, 2)),
            dma((chunks, 8)),
            dma((chunks, 8)),
            dma((chunks, 2)),
            dma((3,)),
        ],
        compiler_params=pltpu.CompilerParams(collective_id=0, has_side_effects=True),
        name="mixing",
    )(tokens, cotangent, first_factor, second_factor)
    scale = 1.0 / jnp.sqrt(jnp.float32(rows * lax.axis_size("dp")))
    first_grad, second_grad = lax.psum((first.astype(F32) * scale, second.astype(F32) * scale), "dp")
    return (output, input_grad, first_grad, second_grad)


def solution(mesh):
    return jax.shard_map(
        shards,
        mesh=mesh,
        in_specs=(P("dp", "mp"), P("dp", "mp"), P("mp", None, None), P("mp", None, None)),
        out_specs=(P("dp", "mp"), P("dp", "mp"), P("mp", None, None), P("mp", None, None)),
        check_vma=False,
    )
```

```python
import jax
import jax.numpy as jnp
from jax import lax
from jax.experimental import pallas as pl
from jax.experimental.pallas import tpu as pltpu
from jax.sharding import PartitionSpec as P

MESH = pl.DeviceIdType.MESH
BF = jnp.bfloat16
F32 = jnp.float32
NT = (((1,), (1,)), ((), ()))
NN = (((1,), (0,)), ((), ()))


def dot(left, right, form=NN):
    return lax.dot_general(left, right, form, preferred_element_type=F32)


def iota(shape, axis):
    return lax.broadcasted_iota(jnp.int32, shape, axis)


def swap_matrix():
    row, col = iota((128, 128), 0), iota((128, 128), 1)
    source = (row & 0b1100111) + ((row & 8) << 1) + ((row & 16) >> 1)
    return (col == source).astype(BF)


def block_of(position, plane):
    above = position >> 5
    absolute = (above + plane) & 1
    return ((position >> 3) & 3) * 16 + absolute * 8 + (position & 7)


def column_ab(code, plane):
    return block_of(code >> 4, plane) * 2 + (code & 1)


def column_ci(code, plane):
    return (code & 1) * 64 + block_of(code >> 4, plane)


def kernel(
    chunks,
    tok, cot, w1, w2,
    out, grad_in, first_out, second_out,
    stage, held, back, landed, xt, gt, w1t, w1p, wpair, wf, wb, sel_ab, sel_ci, acc_first, acc_second, mid,
    part, from_y, piece, from_z, whole, every,
    send_a, recv_a, send_z, recv_z, send_b, recv_b, own_sem, w_send, w_recv, y_send, y_recv, z_send, z_recv, end_send, end_recv,
):
    n = tok.shape[0] // chunks
    d, m = lax.axis_index("dp"), lax.axis_index("mp")
    x, plane, core = m // 4, (m // 2) % 2, m % 2
    me = x * 2 + core
    mate = (d, m + 2 - 4 * plane)
    zl, y = d // 4, d % 4
    scale = 1.0 / jnp.sqrt(jnp.float32(tok.shape[0] * 32))

    def along_y(k):
        q = (y + k) % 4
        return q, (zl * 4 + q, m)

    def along_z(k):
        q = (zl + k) % 8
        return q, (q * 4 + y, m)

    def peer(k):
        q = (me + k) % 8
        return q, (d, (q // 2) * 4 + plane * 2 + q % 2)

    barrier = pltpu.get_barrier_semaphore()
    for k in range(1, 8):
        pl.semaphore_signal(barrier, inc=1, device_id=peer(k)[1], device_id_type=MESH)
    pl.semaphore_signal(barrier, inc=1, device_id=mate, device_id_type=MESH)
    for k in range(1, 4):
        pl.semaphore_signal(barrier, inc=1, device_id=along_y(k)[1], device_id_type=MESH)
    for k in range(1, 8):
        pl.semaphore_signal(barrier, inc=1, device_id=along_z(k)[1], device_id_type=MESH)

    def give_weights():
        return pltpu.make_async_remote_copy(
            w2.at[y], wpair.at[plane, y], w_send.at[0], w_recv.at[0], device_id=mate, device_id_type=MESH
        )

    def pass_weights(k):
        return pltpu.make_async_remote_copy(
            wpair.at[1 - plane, y], wpair.at[1 - plane, y],
            w_send.at[k], w_recv.at[k], device_id=along_y(k)[1], device_id_type=MESH,
        )

    def keep_weights():
        return pltpu.make_async_copy(w2, wpair.at[plane], w_send.at[4])

    def scatter_y(kind, k):
        q, device = along_y(k)
        return pltpu.make_async_remote_copy(
            part.at[kind, q], from_y.at[kind, k], y_send.at[kind, k], y_recv.at[kind, k],
            device_id=device, device_id_type=MESH,
        )

    def scatter_z(kind, k):
        q, device = along_z(k)
        return pltpu.make_async_remote_copy(
            piece.at[kind, q], from_z.at[kind, k], z_send.at[kind, k], z_recv.at[kind, k],
            device_id=device, device_id_type=MESH,
        )

    def gather_z(k):
        return pltpu.make_async_remote_copy(
            whole.at[:, zl], whole.at[:, zl], end_send.at[0, k], end_recv.at[0, k],
            device_id=along_z(k)[1], device_id_type=MESH,
        )

    def gather_y(k):
        return pltpu.make_async_remote_copy(
            whole, every.at[y], end_send.at[1, k], end_recv.at[1, k],
            device_id=along_y(k)[1], device_id_type=MESH,
        )

    def out_copy(c, k):
        q, device = peer(k)
        return pltpu.make_async_remote_copy(
            stage.at[c, q], held.at[c, 0, :, pl.ds(4 * me, 4)],
            send_a.at[c, k], recv_a.at[c, k], device_id=device, device_id_type=MESH,
        )

    def out_own(c):
        return pltpu.make_async_copy(stage.at[c, me], held.at[c, 0, :, pl.ds(4 * me, 4)], own_sem.at[c, 0])

    def plane_copy(c, kind):
        return pltpu.make_async_remote_copy(
            held.at[c, 0, kind], held.at[c, 1, kind],
            send_z.at[c, kind], recv_z.at[c, kind], device_id=mate, device_id_type=MESH,
        )

    def back_copy(c, k):
        q, device = peer(k)
        return pltpu.make_async_remote_copy(
            back.at[c, q], landed.at[c, :, :, me],
            send_b.at[c, k], recv_b.at[c, k], device_id=device, device_id_type=MESH,
        )

    def back_own(c):
        return pltpu.make_async_copy(back.at[c, me], landed.at[c, :, :, me], own_sem.at[c, 1])

    swap = swap_matrix()
    for i in range(4):
        half = dot(swap, w1[i], NT).astype(BF)
        w1t[i] = dot(half, swap).astype(BF)
        half = dot(swap, w1[i]).astype(BF)
        w1p[i] = dot(half, swap).astype(BF)
    acc_first[...] = jnp.zeros_like(acc_first)
    pl.semaphore_wait(barrier, 18)
    give_weights().start()
    keep_weights().start()

    def to_mate(c):
        for k in range(1, 8):
            out_copy(c, k).wait_recv()
        out_own(c).wait()
        for kind in range(2):
            plane_copy(c, kind).start()

    def begin(c, _):
        rows = pl.ds(pl.multiple_of(c * n, n), n)
        for i in range(4):
            cols = pl.ds(128 * i, 128)
            xf = dot(swap, tok[rows, cols], NT)
            gf = dot(swap, cot[rows, cols], NT)
            xb = xf.astype(BF)
            xt[c, i] = xb
            gt[c, i] = gf.astype(BF)
            hidden = dot(w1t[i], xb).astype(BF)
            grad_z = (gf * (xf * jax.nn.sigmoid(xf))).astype(BF)
            stage[c, :, 0, i] = hidden.reshape(8, 16, n)
            stage[c, :, 1, i] = grad_z.reshape(8, 16, n)
        out_own(c).start()
        for k in range(1, 8):
            out_copy(c, k).start()

        @pl.when(c >= 1)
        def _():
            to_mate(c - 1)

        return 0

    lax.fori_loop(0, chunks, begin, 0)
    to_mate(chunks - 1)

    give_weights().wait_recv()
    for k in range(1, 4):
        pass_weights(k).start()

    rows_q, cols_q = iota((128, 1024), 0), iota((128, 1024), 1)
    sel_ab[...] = (rows_q == column_ab(cols_q, plane)).astype(BF)
    sel_ci[...] = (rows_q == column_ci(cols_q, plane)).astype(BF)
    keep_weights().wait()
    for k in range(1, 4):
        pass_weights(k).wait_recv()

    def spread(b, _):
        start = pl.multiple_of(b * 128, 128)
        code = iota((128, 128), 0) + b * 128
        lane = iota((128, 128), 1)
        pick_ab = (lane == column_ab(code, plane)).astype(BF)
        pick_ci = (lane == column_ci(code, plane)).astype(BF)
        group = (code >> 1) & 7
        forward = jnp.zeros((128, 128), F32)
        backward = jnp.zeros((128, 128), F32)
        for j in range(8):
            block = wpair[j // 4, j % 4]
            forward = jnp.where(group == j, dot(pick_ab, block, NT), forward)
            backward = jnp.where(group == j, dot(pick_ci, block), backward)
        same = ((iota((128, 1024), 0) >> 1) & 7) == ((cols_q >> 1) & 7)
        wf[pl.ds(start, 128)] = jnp.where(same, dot(forward.astype(BF), sel_ci[...]), 0.0).astype(BF)
        wb[pl.ds(start, 128)] = jnp.where(same, dot(backward.astype(BF), sel_ab[...]), 0.0).astype(BF)
        return 0

    lax.fori_loop(0, 4, spread, 0)
    acc_second[...] = jnp.zeros_like(acc_second)
    eye = (iota((n, n), 0) == iota((n, n), 1)).astype(BF)

    def finish(c):
        for k in range(1, 8):
            back_copy(c, k).wait_recv()
        back_own(c).wait()
        rows = pl.ds(pl.multiple_of(c * n, n), n)
        for i in range(4):
            cols = pl.ds(128 * i, 128)
            xb = xt[c, i]
            xf = xb.astype(F32)
            gf = gt[c, i].astype(F32)
            zf = landed[c, 0, i].reshape(128, n).astype(F32)
            gu = landed[c, 1, i].reshape(128, n)
            sig = jax.nn.sigmoid(xf)
            y = (zf * (xf * sig)).astype(BF)
            gate = (gf * zf * sig * (1.0 + xf * (1.0 - sig))).astype(BF)
            gx = (dot(w1p[i], gu) + gate.astype(F32)).astype(BF)
            acc_first[i] += dot(xb, gu, NT)
            out[rows, cols] = dot(dot(eye, y, NT).astype(BF), swap).astype(BF)
            grad_in[rows, cols] = dot(dot(eye, gx, NT).astype(BF), swap).astype(BF)

    def middle(c, _):
        for kind in range(2):
            plane_copy(c, kind).wait_recv()
        hidden = held[c, :, 0].reshape(1024, n)
        grad_mixed = held[c, :, 1].reshape(1024, n)
        back[c, :, 0] = dot(wf[...], hidden).astype(BF).reshape(8, 4, 16, n)
        back[c, :, 1] = dot(wb[...], grad_mixed).astype(BF).reshape(8, 4, 16, n)
        back_own(c).start()
        for k in range(1, 8):
            back_copy(c, k).start()
        acc_second[...] += dot(hidden, grad_mixed, NT)

        @pl.when(c >= 1)
        def _():
            finish(c - 1)

        return 0

    lax.fori_loop(0, chunks, middle, 0)

    def gather(b, _):
        start = pl.multiple_of(b * 128, 128)
        code = iota((128, 1024), 0)
        same = ((code >> 1) & 7) == ((cols_q >> 1) & 7)
        part = jnp.where(same, acc_second[pl.ds(start, 128)], 0.0).astype(BF)
        mid[pl.ds(start, 128)] = dot(part, sel_ab[...], NT).astype(BF)
        return 0

    lax.fori_loop(0, 8, gather, 0)
    for j in range(4):
        chosen = ((cols_q >> 1) & 7) == plane * 4 + j
        pick = jnp.where(chosen, sel_ci[...].astype(F32), 0.0).astype(BF)
        part[1, j] = dot(pick, mid[...]).astype(BF)
    for k in range(1, 4):
        scatter_y(1, k).start()
    finish(chunks - 1)
    for i in range(4):
        half = dot(swap, acc_first[i].astype(BF)).astype(BF)
        part[0, i] = dot(half, swap).astype(BF)
    for k in range(1, 4):
        scatter_y(0, k).start()
    for kind in (1, 0):
        total = part[kind, y].astype(F32)
        for k in range(1, 4):
            scatter_y(kind, k).wait_recv()
            total += from_y[kind, k].astype(F32)
        piece[kind] = total.astype(BF).reshape(8, 16, 128)
        for k in range(1, 8):
            scatter_z(kind, k).start()
    for kind in (1, 0):
        total = piece[kind, zl].astype(F32)
        for k in range(1, 8):
            scatter_z(kind, k).wait_recv()
            total += from_z[kind, k].astype(F32)
        whole[kind, zl] = total.astype(BF)
    for k in range(1, 8):
        gather_z(k).start()
    for k in range(1, 8):
        gather_z(k).wait_recv()
    for k in range(1, 4):
        gather_y(k).start()
    first_out[y] = whole[0].reshape(128, 128).astype(F32) * scale
    second_out[y] = whole[1].reshape(128, 128).astype(F32) * scale
    for k in range(1, 4):
        gather_y(k).wait_recv()
        q = (y + 4 - k) % 4
        first_out[q] = every[q, 0].reshape(128, 128).astype(F32) * scale
        second_out[q] = every[q, 1].reshape(128, 128).astype(F32) * scale

    def drain(c, _):
        for k in range(1, 8):
            out_copy(c, k).wait_send()
            back_copy(c, k).wait_send()
        for kind in range(2):
            plane_copy(c, kind).wait_send()
        return 0

    lax.fori_loop(0, chunks, drain, 0)
    give_weights().wait_send()
    for k in range(1, 4):
        pass_weights(k).wait_send()
        scatter_y(0, k).wait_send()
        scatter_y(1, k).wait_send()
        gather_y(k).wait_send()
    for k in range(1, 8):
        scatter_z(0, k).wait_send()
        scatter_z(1, k).wait_send()
        gather_z(k).wait_send()


def shards(tokens, cotangent, first_factor, second_factor):
    rows, width = tokens.shape
    chunks = 8
    n = rows // chunks
    V = pl.BlockSpec(memory_space=pltpu.VMEM)
    dma = pltpu.SemaphoreType.DMA
    small = jax.ShapeDtypeStruct(first_factor.shape, F32)
    wide = jax.ShapeDtypeStruct((rows, width), BF)
    return pl.pallas_call(
        lambda *refs: kernel(chunks, *refs),
        out_shape=(wide, wide, small, small),
        in_specs=[V] * 4,
        out_specs=(V,) * 4,
        scratch_shapes=[
            pltpu.VMEM((chunks, 8, 2, 4, 16, n), BF),
            pltpu.VMEM((chunks, 2, 2, 32, 16, n), BF),
            pltpu.VMEM((chunks, 8, 2, 4, 16, n), BF),
            pltpu.VMEM((chunks, 2, 4, 8, 16, n), BF),
            pltpu.VMEM((chunks, 4, 128, n), BF),
            pltpu.VMEM((chunks, 4, 128, n), BF),
            pltpu.VMEM((4, 128, 128), BF),
            pltpu.VMEM((4, 128, 128), BF),
            pltpu.VMEM((2, 4, 128, 128), BF),
            pltpu.VMEM((512, 1024), BF),
            pltpu.VMEM((512, 1024), BF),
            pltpu.VMEM((128, 1024), BF),
            pltpu.VMEM((128, 1024), BF),
            pltpu.VMEM((4, 128, 128), F32),
            pltpu.VMEM((1024, 1024), F32),
            pltpu.VMEM((1024, 128), BF),
            pltpu.VMEM((2, 4, 128, 128), BF),
            pltpu.VMEM((2, 4, 128, 128), BF),
            pltpu.VMEM((2, 8, 16, 128), BF),
            pltpu.VMEM((2, 8, 16, 128), BF),
            pltpu.VMEM((2, 8, 16, 128), BF),
            pltpu.VMEM((4, 2, 8, 16, 128), BF),
            dma((chunks, 8)),
            dma((chunks, 8)),
            dma((chunks, 2)),
            dma((chunks, 2)),
            dma((chunks, 8)),
            dma((chunks, 8)),
            dma((chunks, 2)),
            dma((5,)),
            dma((4,)),
            dma((2, 4)),
            dma((2, 4)),
            dma((2, 8)),
            dma((2, 8)),
            dma((2, 8)),
            dma((2, 8)),
        ],
        compiler_params=pltpu.CompilerParams(collective_id=0, has_side_effects=True),
        name="mixing",
    )(tokens, cotangent, first_factor, second_factor)


def solution(mesh):
    return jax.shard_map(
        shards,
        mesh=mesh,
        in_specs=(P("dp", "mp"), P("dp", "mp"), P("mp", None, None), P("mp", None, None)),
        out_specs=(P("dp", "mp"), P("dp", "mp"), P("mp", None, None), P("mp", None, None)),
        check_vma=False,
    )
```

```python
import jax
import jax.numpy as jnp
from jax import lax
from jax.experimental import pallas as pl
from jax.experimental.pallas import tpu as pltpu
from jax.sharding import PartitionSpec as P

MESH = pl.DeviceIdType.MESH
BF = jnp.bfloat16
F32 = jnp.float32
NT = (((1,), (1,)), ((), ()))
NN = (((1,), (0,)), ((), ()))


def dot(left, right, form=NN):
    return lax.dot_general(left, right, form, preferred_element_type=F32)


def iota(shape, axis):
    return lax.broadcasted_iota(jnp.int32, shape, axis)


def swap_matrix():
    row, col = iota((128, 128), 0), iota((128, 128), 1)
    source = (row & 0b1100111) + ((row & 8) << 1) + ((row & 16) >> 1)
    return (col == source).astype(BF)


def block_of(position, plane):
    above = position >> 5
    absolute = (above + plane) & 1
    return ((position >> 3) & 3) * 16 + absolute * 8 + (position & 7)


def column_ab(code, plane):
    return block_of(code >> 4, plane) * 2 + (code & 1)


def column_ci(code, plane):
    return (code & 1) * 64 + block_of(code >> 4, plane)


def kernel(
    chunks,
    tok, cot, w1, w2,
    out, grad_in, first_out, second_out,
    stage, held, back, landed, xt, gt, w1t, w1p, wpair, wf, wb, sel_ab, sel_ci, acc_first, acc_second, mid,
    part, from_y, cross, cross_y, other, piece, from_z, whole, every,
    send_a, recv_a, send_z, recv_z, send_b, recv_b, own_sem, w_send, w_recv, y_send, y_recv, z_send, z_recv, end_send, end_recv, swap_sem,
):
    n = tok.shape[0] // chunks
    d, m = lax.axis_index("dp"), lax.axis_index("mp")
    x, plane, core = m // 4, (m // 2) % 2, m % 2
    me = x * 2 + core
    mate = (d, m + 2 - 4 * plane)
    zl, y = d // 4, d % 4
    scale = 1.0 / jnp.sqrt(jnp.float32(tok.shape[0] * lax.axis_size("dp")))

    def along_y(k):
        q = (y + k) % 4
        return q, (zl * 4 + q, m)

    def along_z(k):
        q = (zl + k) % 8
        return q, (q * 4 + y, m)

    def peer(k):
        q = (me + k) % 8
        return q, (d, (q // 2) * 4 + plane * 2 + q % 2)

    barrier = pltpu.get_barrier_semaphore()
    for k in range(1, 8):
        pl.semaphore_signal(barrier, inc=1, device_id=peer(k)[1], device_id_type=MESH)
    pl.semaphore_signal(barrier, inc=1, device_id=mate, device_id_type=MESH)
    for k in range(1, 4):
        pl.semaphore_signal(barrier, inc=1, device_id=along_y(k)[1], device_id_type=MESH)
    for k in range(1, 8):
        pl.semaphore_signal(barrier, inc=1, device_id=along_z(k)[1], device_id_type=MESH)

    def give_weights():
        return pltpu.make_async_remote_copy(
            w2.at[y], wpair.at[plane, y], w_send.at[0], w_recv.at[0], device_id=mate, device_id_type=MESH
        )

    def pass_weights(k):
        return pltpu.make_async_remote_copy(
            wpair.at[1 - plane, y], wpair.at[1 - plane, y],
            w_send.at[k], w_recv.at[k], device_id=along_y(k)[1], device_id_type=MESH,
        )

    def keep_weights():
        return pltpu.make_async_copy(w2, wpair.at[plane], w_send.at[4])

    def scatter_y(kind, k):
        q, device = along_y(k)
        return pltpu.make_async_remote_copy(
            cross.at[:, q] if kind else part.at[q], cross_y.at[k] if kind else from_y.at[k],
            y_send.at[kind, k], y_recv.at[kind, k], device_id=device, device_id_type=MESH,
        )

    def swap_planes():
        return pltpu.make_async_remote_copy(
            other.at[0], other.at[1], swap_sem.at[0], swap_sem.at[1], device_id=mate, device_id_type=MESH
        )

    def scatter_z(kind, k):
        q, device = along_z(k)
        return pltpu.make_async_remote_copy(
            piece.at[kind, q], from_z.at[kind, k], z_send.at[kind, k], z_recv.at[kind, k],
            device_id=device, device_id_type=MESH,
        )

    def gather_z(k):
        return pltpu.make_async_remote_copy(
            whole.at[:, zl], whole.at[:, zl], end_send.at[0, k], end_recv.at[0, k],
            device_id=along_z(k)[1], device_id_type=MESH,
        )

    def gather_y(k):
        return pltpu.make_async_remote_copy(
            whole, every.at[y], end_send.at[1, k], end_recv.at[1, k],
            device_id=along_y(k)[1], device_id_type=MESH,
        )

    def out_copy(c, kind, k):
        q, device = peer(k)
        return pltpu.make_async_remote_copy(
            stage.at[c, kind, q], held.at[c, 0, kind, pl.ds(4 * me, 4)],
            send_a.at[c, kind, k], recv_a.at[c, kind, k], device_id=device, device_id_type=MESH,
        )

    def out_own(c, kind):
        return pltpu.make_async_copy(
            stage.at[c, kind, me], held.at[c, 0, kind, pl.ds(4 * me, 4)], own_sem.at[c, kind]
        )

    def plane_copy(c, kind):
        return pltpu.make_async_remote_copy(
            held.at[c, 0, kind], held.at[c, 1, kind],
            send_z.at[c, kind], recv_z.at[c, kind], device_id=mate, device_id_type=MESH,
        )

    def back_copy(c, kind, k):
        q, device = peer(k)
        return pltpu.make_async_remote_copy(
            back.at[c, kind, q], landed.at[c, kind, :, me],
            send_b.at[c, kind, k], recv_b.at[c, kind, k], device_id=device, device_id_type=MESH,
        )

    def back_own(c, kind):
        return pltpu.make_async_copy(back.at[c, kind, me], landed.at[c, kind, :, me], own_sem.at[c, 2 + kind])

    def send_out(c, kind):
        out_own(c, kind).start()
        for k in range(1, 8):
            out_copy(c, kind, k).start()

    def send_back(c, kind):
        back_own(c, kind).start()
        for k in range(1, 8):
            back_copy(c, kind, k).start()

    def await_back(c, kind):
        for k in range(1, 8):
            back_copy(c, kind, k).wait_recv()
        back_own(c, kind).wait()

    swap = swap_matrix()
    for i in range(4):
        half = dot(swap, w1[i], NT).astype(BF)
        w1t[i] = dot(half, swap).astype(BF)
        half = dot(swap, w1[i]).astype(BF)
        w1p[i] = dot(half, swap).astype(BF)
    acc_first[...] = jnp.zeros_like(acc_first)
    pl.semaphore_wait(barrier, 18)
    give_weights().start()
    keep_weights().start()

    def to_mate(c, kind):
        for k in range(1, 8):
            out_copy(c, kind, k).wait_recv()
        out_own(c, kind).wait()
        plane_copy(c, kind).start()

    def begin(c, _):
        rows = pl.ds(pl.multiple_of(c * n, n), n)
        for i in range(4):
            cols = pl.ds(128 * i, 128)
            xf = dot(swap, tok[rows, cols], NT)
            gf = dot(swap, cot[rows, cols], NT)
            xt[c, i] = xf.astype(BF)
            gt[c, i] = gf.astype(BF)
            grad_z = (gf * (xf * jax.nn.sigmoid(xf))).astype(BF)
            stage[c, 1, :, i] = grad_z.reshape(8, 16, n)
        send_out(c, 1)
        for i in range(4):
            stage[c, 0, :, i] = dot(w1t[i], xt[c, i]).astype(BF).reshape(8, 16, n)
        send_out(c, 0)

        @pl.when(c >= 1)
        def _():
            to_mate(c - 1, 1)

        return 0

    lax.fori_loop(0, chunks, begin, 0)
    to_mate(chunks - 1, 1)
    for c in range(3):
        to_mate(c, 0)

    give_weights().wait_recv()
    for k in range(1, 4):
        pass_weights(k).start()

    rows_q, cols_q = iota((128, 1024), 0), iota((128, 1024), 1)
    sel_ab[...] = (rows_q == column_ab(cols_q, plane)).astype(BF)
    sel_ci[...] = (rows_q == column_ci(cols_q, plane)).astype(BF)
    keep_weights().wait()
    for k in range(1, 4):
        pass_weights(k).wait_recv()

    def spread(b, _):
        start = pl.multiple_of(b * 128, 128)
        code = iota((128, 128), 0) + b * 128
        lane = iota((128, 128), 1)
        pick_ab = (lane == column_ab(code, plane)).astype(BF)
        pick_ci = (lane == column_ci(code, plane)).astype(BF)
        group = (code >> 1) & 7
        forward = jnp.zeros((128, 128), F32)
        backward = jnp.zeros((128, 128), F32)
        for j in range(8):
            block = wpair[j // 4, j % 4]
            forward = jnp.where(group == j, dot(pick_ab, block, NT), forward)
            backward = jnp.where(group == j, dot(pick_ci, block), backward)
        same = ((iota((128, 1024), 0) >> 1) & 7) == ((cols_q >> 1) & 7)
        wf[pl.ds(start, 128)] = jnp.where(same, dot(forward.astype(BF), sel_ci[...]), 0.0).astype(BF)
        wb[pl.ds(start, 128)] = jnp.where(same, dot(backward.astype(BF), sel_ab[...]), 0.0).astype(BF)
        return 0

    lax.fori_loop(0, 4, spread, 0)
    acc_second[...] = jnp.zeros_like(acc_second)
    eye = (iota((n, n), 0) == iota((n, n), 1)).astype(BF)

    def first_term(c):
        await_back(c, 1)
        for i in range(4):
            acc_first[i] += dot(xt[c, i], landed[c, 1, i].reshape(128, n), NT)

    def finish(c):
        await_back(c, 0)
        rows = pl.ds(pl.multiple_of(c * n, n), n)
        for i in range(4):
            cols = pl.ds(128 * i, 128)
            xf = xt[c, i].astype(F32)
            gf = gt[c, i].astype(F32)
            zf = landed[c, 0, i].reshape(128, n).astype(F32)
            gu = landed[c, 1, i].reshape(128, n)
            sig = jax.nn.sigmoid(xf)
            y_part = (zf * (xf * sig)).astype(BF)
            gate = (gf * zf * sig * (1.0 + xf * (1.0 - sig))).astype(BF)
            gx = (dot(w1p[i], gu) + gate.astype(F32)).astype(BF)
            out[rows, cols] = dot(dot(eye, y_part, NT).astype(BF), swap).astype(BF)
            grad_in[rows, cols] = dot(dot(eye, gx, NT).astype(BF), swap).astype(BF)

    def backward(c, _):
        plane_copy(c, 1).wait_recv()
        grad_mixed = held[c, :, 1].reshape(1024, n)
        back[c, 1] = dot(wb[...], grad_mixed).astype(BF).reshape(8, 4, 16, n)
        send_back(c, 1)
        acc_second[...] += dot(held[c, 0, 0].reshape(512, n), grad_mixed, NT)

        @pl.when(c >= 1)
        def _():
            first_term(c - 1)

        return 0

    def forward(c, _):
        plane_copy(c, 0).wait_recv()
        hidden = held[c, :, 0].reshape(1024, n)
        back[c, 0] = dot(wf[...], hidden).astype(BF).reshape(8, 4, 16, n)
        send_back(c, 0)

        @pl.when(c >= 1)
        def _():
            finish(c - 1)

        return 0

    def own_hidden(c, _):
        for k in range(1, 8):
            out_copy(c, 0, k).wait_recv()
        out_own(c, 0).wait()
        return 0

    lax.fori_loop(3, chunks, own_hidden, 0)
    lax.fori_loop(0, chunks, backward, 0)

    def gather(b, _):
        start = pl.multiple_of(b * 128, 128)
        code = iota((128, 1024), 0)
        same = ((code >> 1) & 7) == ((cols_q >> 1) & 7)
        row_part = jnp.where(same, acc_second[pl.ds(start, 128)], 0.0).astype(BF)
        mid[pl.ds(start, 128)] = dot(row_part, sel_ab[...], NT).astype(BF)
        return 0

    lax.fori_loop(0, 4, gather, 0)
    rows_s, cols_s = iota((64, 512), 0), iota((64, 512), 1)
    aligned = ((cols_s >> 4) == (rows_s & 31)) & ((cols_s & 1) == (rows_s >> 5))
    for j in range(8):
        pick = (aligned & (((cols_s >> 1) & 7) == j)).astype(BF)
        cross[j // 4, j % 4] = dot(pick, mid[...]).astype(BF)
    for k in range(1, 4):
        scatter_y(1, k).start()
    first_term(chunks - 1)
    for i in range(4):
        half = dot(swap, acc_first[i].astype(BF)).astype(BF)
        part[i] = dot(half, swap).astype(BF)
    for k in range(1, 4):
        scatter_y(0, k).start()
    kept = cross[plane, y].astype(F32)
    given = cross[1 - plane, y].astype(F32)
    for k in range(1, 4):
        scatter_y(1, k).wait_recv()
        kept += cross_y[k, plane].astype(F32)
        given += cross_y[k, 1 - plane].astype(F32)
    other[0] = given.astype(BF)
    swap_planes().start()
    piece[1, pl.ds(4 * plane, 4)] = kept.astype(BF).reshape(4, 16, 128)
    total = part[y].astype(F32)
    for k in range(1, 4):
        scatter_y(0, k).wait_recv()
        total += from_y[k].astype(F32)
    piece[0] = total.astype(BF).reshape(8, 16, 128)
    for k in range(1, 8):
        scatter_z(0, k).start()
    for c in range(3, 5):
        plane_copy(c, 0).start()
    lax.fori_loop(0, 1, forward, 0)
    swap_planes().wait_recv()
    piece[1, pl.ds(4 - 4 * plane, 4)] = other[1].reshape(4, 16, 128)
    for k in range(1, 8):
        scatter_z(1, k).start()
    plane_copy(5, 0).start()
    lax.fori_loop(1, 2, forward, 0)
    for kind in range(2):
        total = piece[kind, zl].astype(F32)
        for k in range(1, 8):
            scatter_z(kind, k).wait_recv()
            total += from_z[kind, k].astype(F32)
        whole[kind, zl] = total.astype(BF)
    for k in range(1, 8):
        gather_z(k).start()
    for c in range(6, chunks):
        plane_copy(c, 0).start()
    lax.fori_loop(2, 5, forward, 0)
    for k in range(1, 8):
        gather_z(k).wait_recv()
    for k in range(1, 4):
        gather_y(k).start()
    lax.fori_loop(5, 6, forward, 0)

    row, col = iota((128, 128), 0), iota((128, 128), 1)
    ordered = ((row >> 3) & 1) * 64 + (row >> 6) * 32 + ((row >> 4) & 3) * 8 + (row & 7)
    restore = (col == ordered).astype(BF)

    def emit(q, summed):
        first_out[q] = summed[0].reshape(128, 128).astype(F32) * scale
        second_out[q] = dot(restore, summed[1].reshape(128, 128)) * scale

    emit(y, whole)
    for k in range(1, 4):
        gather_y(k).wait_recv()
        q = (y + 4 - k) % 4
        emit(q, every.at[q])
    lax.fori_loop(6, chunks, forward, 0)
    finish(chunks - 1)

    def drain(c, _):
        for k in range(1, 8):
            for kind in range(2):
                out_copy(c, kind, k).wait_send()
                back_copy(c, kind, k).wait_send()
        for kind in range(2):
            plane_copy(c, kind).wait_send()
        return 0

    lax.fori_loop(0, chunks, drain, 0)
    give_weights().wait_send()
    swap_planes().wait_send()
    for k in range(1, 4):
        pass_weights(k).wait_send()
        scatter_y(0, k).wait_send()
        scatter_y(1, k).wait_send()
        gather_y(k).wait_send()
    for k in range(1, 8):
        scatter_z(0, k).wait_send()
        scatter_z(1, k).wait_send()
        gather_z(k).wait_send()


def shards(tokens, cotangent, first_factor, second_factor):
    rows, width = tokens.shape
    chunks = 8
    n = rows // chunks
    V = pl.BlockSpec(memory_space=pltpu.VMEM)
    dma = pltpu.SemaphoreType.DMA
    small = jax.ShapeDtypeStruct(first_factor.shape, F32)
    wide = jax.ShapeDtypeStruct((rows, width), BF)
    return pl.pallas_call(
        lambda *refs: kernel(chunks, *refs),
        out_shape=(wide, wide, small, small),
        in_specs=[V] * 4,
        out_specs=(V,) * 4,
        scratch_shapes=[
            pltpu.VMEM((chunks, 2, 8, 4, 16, n), BF),
            pltpu.VMEM((chunks, 2, 2, 32, 16, n), BF),
            pltpu.VMEM((chunks, 2, 8, 4, 16, n), BF),
            pltpu.VMEM((chunks, 2, 4, 8, 16, n), BF),
            pltpu.VMEM((chunks, 4, 128, n), BF),
            pltpu.VMEM((chunks, 4, 128, n), BF),
            pltpu.VMEM((4, 128, 128), BF),
            pltpu.VMEM((4, 128, 128), BF),
            pltpu.VMEM((2, 4, 128, 128), BF),
            pltpu.VMEM((512, 1024), BF),
            pltpu.VMEM((512, 1024), BF),
            pltpu.VMEM((128, 1024), BF),
            pltpu.VMEM((128, 1024), BF),
            pltpu.VMEM((4, 128, 128), F32),
            pltpu.VMEM((512, 1024), F32),
            pltpu.VMEM((512, 128), BF),
            pltpu.VMEM((4, 128, 128), BF),
            pltpu.VMEM((4, 128, 128), BF),
            pltpu.VMEM((2, 4, 64, 128), BF),
            pltpu.VMEM((4, 2, 64, 128), BF),
            pltpu.VMEM((2, 64, 128), BF),
            pltpu.VMEM((2, 8, 16, 128), BF),
            pltpu.VMEM((2, 8, 16, 128), BF),
            pltpu.VMEM((2, 8, 16, 128), BF),
            pltpu.VMEM((4, 2, 8, 16, 128), BF),
            dma((chunks, 2, 8)),
            dma((chunks, 2, 8)),
            dma((chunks, 2)),
            dma((chunks, 2)),
            dma((chunks, 2, 8)),
            dma((chunks, 2, 8)),
            dma((chunks, 4)),
            dma((5,)),
            dma((4,)),
            dma((2, 4)),
            dma((2, 4)),
            dma((2, 8)),
            dma((2, 8)),
            dma((2, 8)),
            dma((2, 8)),
            dma((2,)),
        ],
        compiler_params=pltpu.CompilerParams(collective_id=0, has_side_effects=True),
        name="mixing",
    )(tokens, cotangent, first_factor, second_factor)


def solution(mesh):
    return jax.shard_map(
        shards,
        mesh=mesh,
        in_specs=(P("dp", "mp"), P("dp", "mp"), P("mp", None, None), P("mp", None, None)),
        out_specs=(P("dp", "mp"), P("dp", "mp"), P("mp", None, None), P("mp", None, None)),
        check_vma=False,
    )
```

```python
import jax
import jax.numpy as jnp
from jax import lax
from jax.experimental import pallas as pl
from jax.experimental.pallas import tpu as pltpu
from jax.sharding import PartitionSpec as P

MESH = pl.DeviceIdType.MESH
BF = jnp.bfloat16
F32 = jnp.float32
NT = (((1,), (1,)), ((), ()))
NN = (((1,), (0,)), ((), ()))


def dot(left, right, form=NN):
    return lax.dot_general(left, right, form, preferred_element_type=F32)


def iota(shape, axis):
    return lax.broadcasted_iota(jnp.int32, shape, axis)


def swap_matrix():
    row, col = iota((128, 128), 0), iota((128, 128), 1)
    source = (row & 0b1100111) + ((row & 8) << 1) + ((row & 16) >> 1)
    return (col == source).astype(BF)


def block_of(position, plane):
    above = position >> 5
    absolute = (above + plane) & 1
    return ((position >> 3) & 3) * 16 + absolute * 8 + (position & 7)


def column_ab(code, plane):
    return block_of(code >> 4, plane) * 2 + (code & 1)


def column_ci(code, plane):
    return (code & 1) * 64 + block_of(code >> 4, plane)


def kernel(
    chunks,
    tok, cot, w1, w2,
    out, grad_in, first_out, second_out,
    stage, held, back, landed, xt, gt, silu, slope, base, w1t, w1p, wpair, wf, wb, sel_ab, sel_ci, acc_first, acc_second, mid,
    part, from_y, cross, cross_y, other, piece, from_z, whole, every,
    send_a, recv_a, send_z, recv_z, send_b, recv_b, own_sem, w_send, w_recv, y_send, y_recv, z_send, z_recv, end_send, end_recv, swap_sem,
):
    n = tok.shape[0] // chunks
    d, m = lax.axis_index("dp"), lax.axis_index("mp")
    x, plane, core = m // 4, (m // 2) % 2, m % 2
    me = x * 2 + core
    mate = (d, m + 2 - 4 * plane)
    zl, y = d // 4, d % 4
    scale = 1.0 / jnp.sqrt(jnp.float32(tok.shape[0] * lax.axis_size("dp")))

    def along_y(k):
        q = (y + k) % 4
        return q, (zl * 4 + q, m)

    def along_z(k):
        q = (zl + k) % 8
        return q, (q * 4 + y, m)

    def peer(k):
        q = (me + k) % 8
        return q, (d, (q // 2) * 4 + plane * 2 + q % 2)

    barrier = pltpu.get_barrier_semaphore()
    for k in range(1, 8):
        pl.semaphore_signal(barrier, inc=1, device_id=peer(k)[1], device_id_type=MESH)
    pl.semaphore_signal(barrier, inc=1, device_id=mate, device_id_type=MESH)
    for k in range(1, 4):
        pl.semaphore_signal(barrier, inc=1, device_id=along_y(k)[1], device_id_type=MESH)
    for k in range(1, 8):
        pl.semaphore_signal(barrier, inc=1, device_id=along_z(k)[1], device_id_type=MESH)

    def give_weights():
        return pltpu.make_async_remote_copy(
            w2.at[y], wpair.at[plane, y], w_send.at[0], w_recv.at[0], device_id=mate, device_id_type=MESH
        )

    def pass_weights(k):
        return pltpu.make_async_remote_copy(
            wpair.at[1 - plane, y], wpair.at[1 - plane, y],
            w_send.at[k], w_recv.at[k], device_id=along_y(k)[1], device_id_type=MESH,
        )

    def keep_weights():
        return pltpu.make_async_copy(w2, wpair.at[plane], w_send.at[4])

    def scatter_y(kind, k):
        q, device = along_y(k)
        return pltpu.make_async_remote_copy(
            cross.at[:, q] if kind else part.at[q], cross_y.at[k] if kind else from_y.at[k],
            y_send.at[kind, k], y_recv.at[kind, k], device_id=device, device_id_type=MESH,
        )

    def swap_planes():
        return pltpu.make_async_remote_copy(
            other.at[0], other.at[1], swap_sem.at[0], swap_sem.at[1], device_id=mate, device_id_type=MESH
        )

    def scatter_z(kind, k):
        q, device = along_z(k)
        return pltpu.make_async_remote_copy(
            piece.at[kind, q], from_z.at[kind, k], z_send.at[kind, k], z_recv.at[kind, k],
            device_id=device, device_id_type=MESH,
        )

    def gather_z(k):
        return pltpu.make_async_remote_copy(
            whole.at[:, zl], whole.at[:, zl], end_send.at[0, k], end_recv.at[0, k],
            device_id=along_z(k)[1], device_id_type=MESH,
        )

    def gather_y(k):
        return pltpu.make_async_remote_copy(
            whole, every.at[y], end_send.at[1, k], end_recv.at[1, k],
            device_id=along_y(k)[1], device_id_type=MESH,
        )

    def out_copy(c, kind, k):
        q, device = peer(k)
        return pltpu.make_async_remote_copy(
            stage.at[c, kind, q], held.at[c, 0, kind, pl.ds(4 * me, 4)],
            send_a.at[c, kind, k], recv_a.at[c, kind, k], device_id=device, device_id_type=MESH,
        )

    def out_own(c, kind):
        return pltpu.make_async_copy(
            stage.at[c, kind, me], held.at[c, 0, kind, pl.ds(4 * me, 4)], own_sem.at[c, kind]
        )

    def plane_copy(c, kind):
        return pltpu.make_async_remote_copy(
            held.at[c, 0, kind], held.at[c, 1, kind],
            send_z.at[c, kind], recv_z.at[c, kind], device_id=mate, device_id_type=MESH,
        )

    def back_copy(c, kind, k):
        q, device = peer(k)
        return pltpu.make_async_remote_copy(
            back.at[c, kind, q], landed.at[c, kind, :, me],
            send_b.at[c, kind, k], recv_b.at[c, kind, k], device_id=device, device_id_type=MESH,
        )

    def back_own(c, kind):
        return pltpu.make_async_copy(back.at[c, kind, me], landed.at[c, kind, :, me], own_sem.at[c, 2 + kind])

    def send_out(c, kind):
        out_own(c, kind).start()
        for k in range(1, 8):
            out_copy(c, kind, k).start()

    def send_back(c, kind):
        back_own(c, kind).start()
        for k in range(1, 8):
            back_copy(c, kind, k).start()

    def await_back(c, kind):
        for k in range(1, 8):
            back_copy(c, kind, k).wait_recv()
        back_own(c, kind).wait()

    swap = swap_matrix()
    for i in range(4):
        half = dot(swap, w1[i], NT).astype(BF)
        w1t[i] = dot(half, swap).astype(BF)
        half = dot(swap, w1[i]).astype(BF)
        w1p[i] = dot(half, swap).astype(BF)
    acc_first[...] = jnp.zeros_like(acc_first)
    keep_weights().start()

    def to_mate(c, kind):
        for k in range(1, 8):
            out_copy(c, kind, k).wait_recv()
        out_own(c, kind).wait()
        plane_copy(c, kind).start()

    def prepare(c):
        rows = pl.ds(pl.multiple_of(c * n, n), n)
        for i in range(4):
            cols = pl.ds(128 * i, 128)
            xf = dot(swap, tok[rows, cols], NT)
            gf = dot(swap, cot[rows, cols], NT)
            xt[c, i] = xf.astype(BF)
            gt[c, i] = gf.astype(BF)
            grad_z = (gf * (xf * jax.nn.sigmoid(xf))).astype(BF)
            stage[c, 1, :, i] = grad_z.reshape(8, 16, n)

    def prepare_hidden(c):
        for i in range(4):
            stage[c, 0, :, i] = dot(w1t[i], xt[c, i]).astype(BF).reshape(8, 16, n)

    def begin(c, _):
        prepare(c)
        send_out(c, 1)
        prepare_hidden(c)
        send_out(c, 0)
        to_mate(c - 1, 1)
        return 0

    prepare(0)
    prepare_hidden(0)
    pl.semaphore_wait(barrier, 18)
    send_out(0, 1)
    give_weights().start()
    send_out(0, 0)
    lax.fori_loop(1, chunks, begin, 0)
    to_mate(chunks - 1, 1)
    for c in range(2):
        to_mate(c, 0)

    give_weights().wait_recv()
    for k in range(1, 4):
        pass_weights(k).start()

    rows_q, cols_q = iota((128, 1024), 0), iota((128, 1024), 1)
    sel_ab[...] = (rows_q == column_ab(cols_q, plane)).astype(BF)
    sel_ci[...] = (rows_q == column_ci(cols_q, plane)).astype(BF)
    keep_weights().wait()
    for k in range(1, 4):
        pass_weights(k).wait_recv()

    def spread(b, _):
        start = pl.multiple_of(b * 128, 128)
        code = iota((128, 128), 0) + b * 128
        lane = iota((128, 128), 1)
        pick_ab = (lane == column_ab(code, plane)).astype(BF)
        pick_ci = (lane == column_ci(code, plane)).astype(BF)
        group = (code >> 1) & 7
        forward = jnp.zeros((128, 128), F32)
        backward = jnp.zeros((128, 128), F32)
        for j in range(8):
            block = wpair[j // 4, j % 4]
            forward = jnp.where(group == j, dot(pick_ab, block, NT), forward)
            backward = jnp.where(group == j, dot(pick_ci, block), backward)
        same = ((iota((128, 1024), 0) >> 1) & 7) == ((cols_q >> 1) & 7)
        wf[pl.ds(start, 128)] = jnp.where(same, dot(forward.astype(BF), sel_ci[...]), 0.0).astype(BF)
        wb[pl.ds(start, 128)] = jnp.where(same, dot(backward.astype(BF), sel_ab[...]), 0.0).astype(BF)
        return 0

    lax.fori_loop(0, 4, spread, 0)
    acc_second[...] = jnp.zeros_like(acc_second)
    eye = (iota((n, n), 0) == iota((n, n), 1)).astype(BF)

    def first_term(c):
        await_back(c, 1)
        for i in range(4):
            gu = landed[c, 1, i].reshape(128, n)
            acc_first[i] += dot(xt[c, i], gu, NT)
            base[c, i] = dot(w1p[i], gu)
            xf = xt[c, i].astype(F32)
            sig = jax.nn.sigmoid(xf)
            silu[c, i] = xf * sig
            slope[c, i] = gt[c, i].astype(F32) * sig * (1.0 + xf * (1.0 - sig))

    def finish(c):
        await_back(c, 0)
        rows = pl.ds(pl.multiple_of(c * n, n), n)
        for i in range(4):
            cols = pl.ds(128 * i, 128)
            zf = landed[c, 0, i].reshape(128, n).astype(F32)
            y_part = (zf * silu[c, i]).astype(BF)
            gate = (zf * slope[c, i]).astype(BF)
            gx = (base[c, i] + gate.astype(F32)).astype(BF)
            out[rows, cols] = dot(dot(eye, y_part, NT).astype(BF), swap).astype(BF)
            grad_in[rows, cols] = dot(dot(eye, gx, NT).astype(BF), swap).astype(BF)

    def backward(c, _):
        plane_copy(c, 1).wait_recv()
        grad_mixed = held[c, :, 1].reshape(1024, n)
        back[c, 1] = dot(wb[...], grad_mixed).astype(BF).reshape(8, 4, 16, n)
        send_back(c, 1)
        acc_second[...] += dot(held[c, 0, 0].reshape(512, n), grad_mixed, NT)

        @pl.when(c >= 1)
        def _():
            first_term(c - 1)

        return 0

    def forward(c, _):
        plane_copy(c, 0).wait_recv()
        hidden = held[c, :, 0].reshape(1024, n)
        back[c, 0] = dot(wf[...], hidden).astype(BF).reshape(8, 4, 16, n)
        send_back(c, 0)

        @pl.when(c >= 1)
        def _():
            finish(c - 1)

        return 0

    def own_hidden(c, _):
        for k in range(1, 8):
            out_copy(c, 0, k).wait_recv()
        out_own(c, 0).wait()
        return 0

    lax.fori_loop(2, chunks, own_hidden, 0)
    lax.fori_loop(0, chunks, backward, 0)

    def gather(b, _):
        start = pl.multiple_of(b * 128, 128)
        code = iota((128, 1024), 0)
        same = ((code >> 1) & 7) == ((cols_q >> 1) & 7)
        row_part = jnp.where(same, acc_second[pl.ds(start, 128)], 0.0).astype(BF)
        mid[pl.ds(start, 128)] = dot(row_part, sel_ab[...], NT).astype(BF)
        return 0

    lax.fori_loop(0, 4, gather, 0)
    rows_s, cols_s = iota((64, 512), 0), iota((64, 512), 1)
    aligned = ((cols_s >> 4) == (rows_s & 31)) & ((cols_s & 1) == (rows_s >> 5))
    for j in range(8):
        pick = (aligned & (((cols_s >> 1) & 7) == j)).astype(BF)
        cross[j // 4, j % 4] = dot(pick, mid[...]).astype(BF)
    for k in range(1, 4):
        scatter_y(1, k).start()
    first_term(chunks - 1)
    for i in range(4):
        half = dot(swap, acc_first[i].astype(BF)).astype(BF)
        part[i] = dot(half, swap).astype(BF)
    for k in range(1, 4):
        scatter_y(0, k).start()
    kept = cross[plane, y].astype(F32)
    given = cross[1 - plane, y].astype(F32)
    for k in range(1, 4):
        scatter_y(1, k).wait_recv()
        kept += cross_y[k, plane].astype(F32)
        given += cross_y[k, 1 - plane].astype(F32)
    other[0] = given.astype(BF)
    swap_planes().start()
    piece[1, pl.ds(4 * plane, 4)] = kept.astype(BF).reshape(4, 16, 128)
    total = part[y].astype(F32)
    for k in range(1, 4):
        scatter_y(0, k).wait_recv()
        total += from_y[k].astype(F32)
    piece[0] = total.astype(BF).reshape(8, 16, 128)
    for k in range(1, 8):
        scatter_z(0, k).start()
    for c in range(2, 4):
        plane_copy(c, 0).start()
    lax.fori_loop(0, 1, forward, 0)
    swap_planes().wait_recv()
    piece[1, pl.ds(4 - 4 * plane, 4)] = other[1].reshape(4, 16, 128)
    for k in range(1, 8):
        scatter_z(1, k).start()
    plane_copy(4, 0).start()
    lax.fori_loop(1, 2, forward, 0)
    for kind in range(2):
        total = piece[kind, zl].astype(F32)
        for k in range(1, 8):
            scatter_z(kind, k).wait_recv()
            total += from_z[kind, k].astype(F32)
        whole[kind, zl] = total.astype(BF)
    for k in range(1, 8):
        gather_z(k).start()
    for c in range(5, chunks):
        plane_copy(c, 0).start()
    lax.fori_loop(2, 4, forward, 0)
    for k in range(1, 8):
        gather_z(k).wait_recv()
    for k in range(1, 4):
        gather_y(k).start()
    lax.fori_loop(4, 5, forward, 0)

    row, col = iota((128, 128), 0), iota((128, 128), 1)
    ordered = ((row >> 3) & 1) * 64 + (row >> 6) * 32 + ((row >> 4) & 3) * 8 + (row & 7)
    restore = (col == ordered).astype(BF)

    def emit(q, summed):
        first_out[q] = summed[0].reshape(128, 128).astype(F32) * scale
        second_out[q] = dot(restore, summed[1].reshape(128, 128)) * scale

    emit(y, whole)
    for k in range(1, 4):
        gather_y(k).wait_recv()
        q = (y + 4 - k) % 4
        emit(q, every.at[q])
    lax.fori_loop(5, chunks, forward, 0)
    finish(chunks - 1)

    def drain(c, _):
        for k in range(1, 8):
            for kind in range(2):
                out_copy(c, kind, k).wait_send()
                back_copy(c, kind, k).wait_send()
        for kind in range(2):
            plane_copy(c, kind).wait_send()
        return 0

    lax.fori_loop(0, chunks, drain, 0)
    give_weights().wait_send()
    swap_planes().wait_send()
    for k in range(1, 4):
        pass_weights(k).wait_send()
        scatter_y(0, k).wait_send()
        scatter_y(1, k).wait_send()
        gather_y(k).wait_send()
    for k in range(1, 8):
        scatter_z(0, k).wait_send()
        scatter_z(1, k).wait_send()
        gather_z(k).wait_send()


def shards(tokens, cotangent, first_factor, second_factor):
    rows, width = tokens.shape
    chunks = 8
    n = rows // chunks
    V = pl.BlockSpec(memory_space=pltpu.VMEM)
    dma = pltpu.SemaphoreType.DMA
    small = jax.ShapeDtypeStruct(first_factor.shape, F32)
    wide = jax.ShapeDtypeStruct((rows, width), BF)
    return pl.pallas_call(
        lambda *refs: kernel(chunks, *refs),
        out_shape=(wide, wide, small, small),
        in_specs=[V] * 4,
        out_specs=(V,) * 4,
        scratch_shapes=[
            pltpu.VMEM((chunks, 2, 8, 4, 16, n), BF),
            pltpu.VMEM((chunks, 2, 2, 32, 16, n), BF),
            pltpu.VMEM((chunks, 2, 8, 4, 16, n), BF),
            pltpu.VMEM((chunks, 2, 4, 8, 16, n), BF),
            pltpu.VMEM((chunks, 4, 128, n), BF),
            pltpu.VMEM((chunks, 4, 128, n), BF),
            pltpu.VMEM((chunks, 4, 128, n), F32),
            pltpu.VMEM((chunks, 4, 128, n), F32),
            pltpu.VMEM((chunks, 4, 128, n), F32),
            pltpu.VMEM((4, 128, 128), BF),
            pltpu.VMEM((4, 128, 128), BF),
            pltpu.VMEM((2, 4, 128, 128), BF),
            pltpu.VMEM((512, 1024), BF),
            pltpu.VMEM((512, 1024), BF),
            pltpu.VMEM((128, 1024), BF),
            pltpu.VMEM((128, 1024), BF),
            pltpu.VMEM((4, 128, 128), F32),
            pltpu.VMEM((512, 1024), F32),
            pltpu.VMEM((512, 128), BF),
            pltpu.VMEM((4, 128, 128), BF),
            pltpu.VMEM((4, 128, 128), BF),
            pltpu.VMEM((2, 4, 64, 128), BF),
            pltpu.VMEM((4, 2, 64, 128), BF),
            pltpu.VMEM((2, 64, 128), BF),
            pltpu.VMEM((2, 8, 16, 128), BF),
            pltpu.VMEM((2, 8, 16, 128), BF),
            pltpu.VMEM((2, 8, 16, 128), BF),
            pltpu.VMEM((4, 2, 8, 16, 128), BF),
            dma((chunks, 2, 8)),
            dma((chunks, 2, 8)),
            dma((chunks, 2)),
            dma((chunks, 2)),
            dma((chunks, 2, 8)),
            dma((chunks, 2, 8)),
            dma((chunks, 4)),
            dma((5,)),
            dma((4,)),
            dma((2, 4)),
            dma((2, 4)),
            dma((2, 8)),
            dma((2, 8)),
            dma((2, 8)),
            dma((2, 8)),
            dma((2,)),
        ],
        compiler_params=pltpu.CompilerParams(collective_id=0, has_side_effects=True),
        name="mixing",
    )(tokens, cotangent, first_factor, second_factor)


def solution(mesh):
    return jax.shard_map(
        shards,
        mesh=mesh,
        in_specs=(P("dp", "mp"), P("dp", "mp"), P("mp", None, None), P("mp", None, None)),
        out_specs=(P("dp", "mp"), P("dp", "mp"), P("mp", None, None), P("mp", None, None)),
        check_vma=False,
    )
```
